512 devices in a mesh: blade: 256 (over z, y, x), inst: 2 (over core).
Axes of the slice: x: 4, y: 8, z: 8, core: 2. Of those that a mesh axis runs over, the one named last changes fastest.
Arguments:
- tangent_seed: float32 [256, 5, 24, 1024], P('blade', None, 'inst'), may hold values from -6 to 6
- adjoint_seed: float32 [256, 5, 24, 1024], P('blade', None, 'inst'), may hold values from -6 to 6
- jacobian: bfloat16 [256, 24, 25, 1024], P('blade', 'inst'), may hold values from -1 to 4
- precond: bfloat16 [256, 24, 25, 1024], P('blade', 'inst'), may hold values from -1 to 4
- upwind: float32 [256, 1024], P('blade'), may hold values from 0.2 to 1
- up_weight: float32 [256, 256], P('blade'), may hold values from 0.3 to 1.2
- bottom_face_strength: float32 [256, 256], P('blade'), may hold values from 0.3 to 1.2
- up_cells: int32 [256], replicated, may hold values from 0 to 1023, as said below
- lo_cells: int32 [256], replicated, may hold values from 0 to 1023, as said below
- phase_index: int32 [11], replicated, may hold values from 0 to 255
Outputs:
- tangent_out: float32 [256, 5, 24, 1024], P('blade', None, 'inst')
- adjoint_out: float32 [256, 5, 24, 1024], P('blade', None, 'inst')
The draws below stay inside these ranges and needn't reach their ends.
Inputs may be any that keep to these rules, and one draw needn't show every extreme that they name: `up_cells`: entry f of the table is one of the cells 4 f to 4 f + 3. `lo_cells`: entry f of the table is one of the cells 4 f to 4 f + 3.
All inputs are finite; a program needn't handle non-finite values.
Results may differ from the reference program's by a relative error of at most 0.0003.
Values sent between devices are 32-bit elements; how exact they have to be, the bound alone decides.
No kernel may reach another device: no remote copies, remote signals or barrier semaphores. Data moves between devices by JAX's collectives and lax.ppermute only.
A program may use at most 64 MiB of HBM per device.

```python
import math
import jax
import jax.numpy as jnp
from jax import lax

CELLS = 1024
SNAPSHOT_COUNT = 24
NV = 5
NH = 11
FACE = 256
P_SIZE = 256


def block_law(key):
    key_diag, key_off = jax.random.split(key)
    full_shape = (P_SIZE, SNAPSHOT_COUNT, NV, NV, CELLS)
    equation_slot_number = lax.broadcasted_iota(jnp.int32, full_shape, 2)
    column_position_index = lax.broadcasted_iota(jnp.int32, full_shape, 3)
    identity_mask = (equation_slot_number == column_position_index).astype(jnp.float32)
    diagonal = jnp.exp(jax.random.uniform(key_diag, full_shape, jnp.float32, math.log(1.5), math.log(4.0)))
    coupling = jnp.clip(0.3 * jax.random.normal(key_off, full_shape, jnp.float32), -1.0, 1.0)
    blocks = identity_mask * diagonal + (1.0 - identity_mask) * coupling
    return blocks.reshape((P_SIZE, SNAPSHOT_COUNT, NV * NV, CELLS))


def draw_jacobian(key, part):
    return block_law(jax.random.fold_in(key, 11)).astype(jnp.bfloat16)


def draw_precond(key, part):
    return block_law(jax.random.fold_in(key, 23)).astype(jnp.bfloat16)


def face_table(key):
    within = jax.random.randint(key, (FACE,), 0, 4).astype(jnp.int32)
    within = within.at[0].set(0).at[FACE - 1].set(3)
    return jnp.arange(FACE, dtype=jnp.int32) * 4 + within


def draw_up_cells(key, part):
    return face_table(jax.random.fold_in(key, 5))


def draw_lo_cells(key, part):
    return face_table(jax.random.fold_in(key, 7))


def draw_phase_index(key, part):
    random_generator_seed, key_high, key_low = jax.random.split(jax.random.fold_in(key, 3), 3)
    slot_numbers = jax.random.randint(random_generator_seed, (NH,), 0, P_SIZE).astype(jnp.int32)
    high_slot = jax.random.randint(key_high, (), 0, NH).astype(jnp.int32)
    low_slot = jnp.mod(high_slot + 1 + jax.random.randint(key_low, (), 0, NH - 1).astype(jnp.int32), NH)
    return slot_numbers.at[high_slot].set(P_SIZE - 1).at[low_slot].set(0)


def block_levels(stream_key, shape, cuts, least, top_value):
    level, own = 1.0, jax.random.fold_in(stream_key, 6)
    for position, shards_of in cuts:
        draws = jnp.exp(jax.random.uniform(jax.random.fold_in(own, position), (shards_of,), jnp.float32, least / len(cuts), top_value / len(cuts)))
        level = level * jnp.repeat(draws, shape[position] // shards_of).reshape([-1 if axis == position else 1 for axis in range(len(shape))])
    return level


def bell_draw(stream_key, shape, spread, limit, pieces=(), kind=jnp.bfloat16):
    result = jax.random.normal(stream_key, shape, jnp.float32) * spread
    if len(pieces) > 0:
        result = block_levels(stream_key, shape, pieces, -0.22, 0.18) * result
    return jnp.clip(result, min=-limit, max=limit).astype(kind)


def setup_inputs(seed: int = 0) -> dict:
    keys = jax.random.split(jax.random.key(seed), 11)
    tangent_seed = bell_draw(keys[0], (P_SIZE, NV, SNAPSHOT_COUNT, CELLS), 1.0, 6.0, ((0, 256), (2, 2)), jnp.float32)
    adjoint_seed = bell_draw(keys[1], (P_SIZE, NV, SNAPSHOT_COUNT, CELLS), 1.0, 6.0, ((0, 256), (2, 2)), jnp.float32)
    jacobian = draw_jacobian(jax.random.fold_in(keys[10], 71), 0)
    precond = draw_precond(jax.random.fold_in(keys[10], 71), 0)
    upwind = jnp.clip(jnp.exp(math.log(1.0) - 1.609438 * jax.random.uniform(keys[4], (P_SIZE, CELLS), jnp.float32) ** block_levels(keys[4], (P_SIZE, CELLS), ((0, 256),), -0.2, 0.2)), 0.2, 1.0)
    up_weight = jnp.clip(jnp.exp(math.log(1.2) - 1.3862944 * jax.random.uniform(keys[5], (P_SIZE, FACE), jnp.float32) ** block_levels(keys[5], (P_SIZE, FACE), ((0, 256),), -0.2, 0.2)), 0.3, 1.2)
    bottom_face_strength = jnp.clip(jnp.exp(math.log(1.2) - 1.3862944 * jax.random.uniform(keys[6], (P_SIZE, FACE), jnp.float32) ** block_levels(keys[6], (P_SIZE, FACE), ((0, 256),), -0.2, 0.2)), 0.3, 1.2)
    up_cells = draw_up_cells(jax.random.fold_in(keys[10], 71), 0)
    lo_cells = draw_lo_cells(jax.random.fold_in(keys[10], 71), 0)
    phase_index = draw_phase_index(jax.random.fold_in(keys[10], 71), 0)
    return {"tangent_seed": tangent_seed, "adjoint_seed": adjoint_seed, "jacobian": jacobian, "precond": precond, "upwind": upwind, "up_weight": up_weight, "bottom_face_strength": bottom_face_strength, "up_cells": up_cells, "lo_cells": lo_cells, "phase_index": phase_index}


OMEGA = 0.15


def spectral(phase_index, passages):
    sampled_moments = jnp.arange(SNAPSHOT_COUNT, dtype=jnp.int32)
    snapshot_displacement = sampled_moments[:, None] - sampled_moments[None, :]
    orders = jnp.arange(1, NH + 1, dtype=jnp.int32)
    wrapped = jnp.mod(orders[:, None, None] * snapshot_displacement[None, :, :], SNAPSHOT_COUNT).astype(jnp.float32) / SNAPSHOT_COUNT
    weights = orders.astype(jnp.float32)[:, None, None]
    skewed = -(2.0 / SNAPSHOT_COUNT) * jnp.sum(weights * jnp.sin(2.0 * jnp.pi * wrapped), axis=0)
    derivative = 0.5 * skewed - 0.5 * skewed.T
    phase_angle = phase_index.astype(jnp.float32)[:, None, None] / passages
    parity = 1.0 - 2.0 * jnp.mod(snapshot_displacement, 2).astype(jnp.float32)
    rotation = (1.0 + parity) / SNAPSHOT_COUNT + (2.0 / SNAPSHOT_COUNT) * jnp.sum(jnp.cos(2.0 * jnp.pi * (wrapped - phase_angle)), axis=0)
    return derivative, rotation


def block_apply(blocks, vector):
    variables = vector.shape[1]
    result_rows = []
    for row_index in range(variables):
        summed = blocks[:, :, row_index * variables, :] * vector[:, 0]
        for column_index in range(1, variables):
            summed = summed + blocks[:, :, row_index * variables + column_index, :] * vector[:, column_index]
        result_rows.append(summed)
    return jnp.stack(result_rows, axis=1)


def block_apply_t(blocks, vector):
    variables = vector.shape[1]
    result_rows = []
    for column_index in range(variables):
        summed = blocks[:, :, column_index, :] * vector[:, 0]
        for row_index in range(1, variables):
            summed = summed + blocks[:, :, row_index * variables + column_index, :] * vector[:, row_index]
        result_rows.append(summed)
    return jnp.stack(result_rows, axis=1)


def instance_mix(matrix, vector):
    return jnp.einsum('ts,pvsc->pvtc', matrix, vector, precision=lax.Precision.HIGHEST)


def reference(tangent_seed, adjoint_seed, jacobian, precond, upwind, up_weight, bottom_face_strength, up_cells, lo_cells, phase_index):
    derivative, rotation = spectral(phase_index, P_SIZE)
    padding = ((0, 0), (0, 0), (0, 0), (1, 0))
    rot_lo = instance_mix(rotation, tangent_seed[..., lo_cells])
    rot_up = instance_mix(rotation.T, tangent_seed[..., up_cells])
    shifted = jnp.pad(tangent_seed[..., :-1], padding)
    applied = block_apply(jacobian, tangent_seed) - upwind[:, None, None, :] * shifted + OMEGA * instance_mix(derivative, tangent_seed)
    applied = applied.at[..., up_cells].add(-up_weight[:, None, None, :] * jnp.roll(rot_lo, -1, axis=0))
    applied = applied.at[..., lo_cells].add(-bottom_face_strength[:, None, None, :] * jnp.roll(rot_up, 1, axis=0))
    tangent_out = block_apply(precond, applied)
    dual_field = block_apply_t(precond, adjoint_seed)
    rot_lo = instance_mix(rotation, dual_field[..., lo_cells])
    rot_up = instance_mix(rotation.T, dual_field[..., up_cells])
    shifted = jnp.pad((upwind[:, None, None, :] * dual_field)[..., 1:], ((0, 0), (0, 0), (0, 0), (0, 1)))
    adjoint_out = block_apply_t(jacobian, dual_field) - shifted + OMEGA * instance_mix(derivative.T, dual_field)
    adjoint_out = adjoint_out.at[..., lo_cells].add(-jnp.roll(up_weight[:, None, None, :] * rot_up, 1, axis=0))
    adjoint_out = adjoint_out.at[..., up_cells].add(-jnp.roll(bottom_face_strength[:, None, None, :] * rot_lo, -1, axis=0))
    return tangent_out, adjoint_out
```

```python
import math

import jax
import jax.numpy as jnp
from jax import lax
from jax.experimental import pallas as pl
from jax.experimental.pallas import tpu as pltpu
from jax.sharding import PartitionSpec as P

SNAPS = 24
NH = 11
NV = 5
OWN = 12
OMEGA = 0.15
SUB, LANE = 8, 128
ROWS = NV * OWN
FIELD = 2 * ROWS
FACE_ROWS = 3 * OWN
MPITCH = OWN * 32
CHUNKS = 4
CHUNK = OWN // CHUNKS


def derivative_weights():
    weights = [0.0]
    for n in range(1, 12):
        total = sum(k * math.sin(2 * math.pi * ((k * n) % SNAPS) / SNAPS) for k in range(1, NH + 1))
        weights.append(-(2.0 / SNAPS) * total)
    return weights


DERIV = derivative_weights()


def passed_along(block, axis, distance):
    count = lax.axis_size(axis)
    route = [((i - distance) % count, i) for i in range(count)]
    return lax.ppermute(block, axis, route)


def lanes():
    return lax.broadcasted_iota(jnp.int32, (SUB, LANE), 1)


def sublanes():
    return lax.broadcasted_iota(jnp.int32, (SUB, LANE), 0)


def take(x, index):
    return jnp.take_along_axis(x, index, axis=1, mode="promise_in_bounds")


def quarters(row):
    first = jnp.broadcast_to(row[:, :LANE], (SUB, LANE))
    second = jnp.broadcast_to(row[:, LANE:], (SUB, LANE))
    sub = sublanes()
    both = jnp.where(sub < 4, first, second)
    return take(both, 32 * (sub & 3) + (lanes() & 31))


def wide(row):
    return jnp.concatenate([row[:, LANE * k : LANE * (k + 1)] for k in range(SUB)], axis=0)


def load_blocks(blocks, scratch, first, count):
    def body(t, carry):
        for k in range(SUB):
            tile = blocks[0, t, :, LANE * k : LANE * (k + 1)].astype(jnp.float32)
            scratch[pl.ds(pl.multiple_of(k * MPITCH + t * 32, 8), NV * NV), :] = tile
        return carry

    lax.fori_loop(first, first + count, body, 0)


def fetch(pairs, sems):
    copies = [pltpu.make_async_copy(src, dst, sems.at[n]) for n, (src, dst) in enumerate(pairs)]
    for copy in copies:
        copy.start()
    return copies


def fetch_blocks(blocks, scratch, sems):
    return fetch(
        [(blocks.at[:, pl.ds(CHUNK * n, CHUNK)], scratch.at[:, pl.ds(CHUNK * n, CHUNK)]) for n in range(CHUNKS)],
        sems,
    )


def block_row(scratch, t, ij):
    return scratch[pl.ds(t * 32 + ij, SUB, stride=MPITCH), :]


def packed(parts, quarter):
    result = parts[-1]
    for g in reversed(range(len(parts) - 1)):
        result = jnp.where(quarter == g, parts[g], result)
    return result


def dual_kernel(tangent, adjoint, precond, out, m_s, p_v, a_v, t_sem, p_sem):
    seeds = fetch([(adjoint, a_v), (tangent, out.at[pl.ds(0, ROWS)])], t_sem)
    chunks = fetch_blocks(precond, p_v, p_sem)

    def body(t, carry):
        seed = [a_v[i * OWN + t] for i in range(NV)]
        for j in range(NV):
            total = block_row(m_s, t, j) * seed[0]
            for i in range(1, NV):
                total = total + block_row(m_s, t, i * NV + j) * seed[i]
            out[ROWS + j * OWN + t] = total
        return carry

    for n in range(CHUNKS):
        chunks[n].wait()
        load_blocks(p_v, m_s, CHUNK * n, CHUNK)
        if n == 0:
            seeds[0].wait()
        lax.fori_loop(CHUNK * n, CHUNK * (n + 1), body, 0)
    seeds[1].wait()


def rotate_kernel(
    phase, gathered, up_weight, lo_weight, up_cells, lo_cells,
    up_out, lo_out, g_v, uw, lw, uc, lc, rho, u_s, l_s, sems,
):
    own = lax.axis_index("inst")
    copies = fetch(
        [(up_weight, uw), (lo_weight, lw), (up_cells, uc), (lo_cells, lc), (gathered, g_v)], sems
    )
    shape = (16, LANE)
    order = lax.broadcasted_iota(jnp.int32, shape, 0) + 1
    lag = lax.broadcasted_iota(jnp.int32, shape, 1)
    index = jnp.zeros(shape, jnp.int32)
    for k in range(NH):
        index = jnp.where(order == k + 1, phase[k], index)
    turns = (32 * order * (lag & 31) - 3 * index).astype(jnp.float32)
    turns = turns - 768.0 * jnp.floor(turns * (1.0 / 768.0) + 0.5)
    waves = jnp.where(order <= NH, jnp.cos(turns * (2.0 * math.pi / 768.0)), 0.0)
    parity = (1 - (lag[:1] & 1)).astype(jnp.float32)
    row = (2.0 / SNAPS) * (parity + jnp.sum(waves, axis=0, keepdims=True))
    for n in range(SNAPS):
        rho[n] = jnp.broadcast_to(row[:, n : n + 1], (SUB, LANE))
    for copy in copies[:4]:
        copy.wait()
    quarter = lanes() >> 5
    odd = (quarter & 1) == 1
    up_index = quarters(uc[...]) & (LANE - 1)
    lo_index = quarters(lc[...]) & (LANE - 1)
    even_rows = jnp.where(odd, lo_index, up_index)
    odd_rows = jnp.where(odd, up_index, lo_index)
    up_scale = quarters(uw[...])
    lo_scale = quarters(lw[...])
    up_mid = jnp.where(quarter == 0, 1.0, up_scale)
    lo_mid = jnp.where(quarter == 1, 1.0, lo_scale)
    copies[4].wait()

    def pick(n, carry):
        which = n // OWN
        t = n - OWN * which
        core = jnp.where(which == 0, own, 1 - own)
        rows = [
            take(g_v[core, q * OWN + t], odd_rows if q % 2 else even_rows) for q in range(2 * NV)
        ]
        swapped = [rows[q ^ 1] for q in range(2 * NV)]
        for j in range(3):
            u_s[j, n] = packed(rows[4 * j : 4 * j + 4], quarter)
            l_s[j, n] = packed(swapped[4 * j : 4 * j + 4], quarter)
        return carry

    lax.fori_loop(0, SNAPS, pick, 0)
    for result, source, sign, mid, last in (
        (up_out, u_s, -1, up_mid, up_scale),
        (lo_out, l_s, 1, lo_mid, lo_scale),
    ):
        for j in range(3):
            sums = [None] * OWN
            for s in range(SNAPS):
                x = source[j, s]
                for r in range(OWN):
                    term = rho[(sign * (r - s)) % SNAPS] * x
                    sums[r] = term if sums[r] is None else sums[r] + term
            for r in range(OWN):
                result[OWN * j + r] = sums[r] if j == 0 else sums[r] * (mid if j == 1 else last)


def local_kernel(gathered, jacobian, upwind, out, g_v, j_v, f_v, m_s, mix, g_sem, j_sem):
    own = lax.axis_index("inst")
    fields = fetch([(gathered, g_v), (upwind, f_v)], g_sem)
    chunks = fetch_blocks(jacobian, j_v, j_sem)
    fields[0].wait()

    for fld, sign in ((0, 1.0), (1, -1.0)):

        def mix_body(i, carry):
            base = (fld * NV + i) * OWN
            mine = [g_v[own, base + s] for s in range(OWN)]
            theirs = [g_v[1 - own, base + s] for s in range(OWN)]
            ring = mine + theirs
            for r in range(OWN):
                total = None
                for k in range(1, OWN):
                    term = (sign * OMEGA * DERIV[k]) * (ring[(r - k) % SNAPS] - ring[(r + k) % SNAPS])
                    total = term if total is None else total + term
                mix[base + r] = total
            return carry

        lax.fori_loop(0, NV, mix_body, 0)

    fields[1].wait()
    lane = lanes()
    cell = sublanes() * LANE + lane
    flow = jnp.where(cell == 0, 0.0, wide(f_v[...]))

    def body(t, carry):
        tangent = [g_v[own, i * OWN + t] for i in range(NV)]
        dual = [g_v[own, (NV + i) * OWN + t] for i in range(NV)]
        sums = [None] * NV
        dsums = [None] * NV
        for i in range(NV):
            for j in range(NV):
                m = block_row(m_s, t, i * NV + j)
                term = m * tangent[j]
                sums[i] = term if j == 0 else sums[i] + term
                term = m * dual[i]
                dsums[j] = term if i == 0 else dsums[j] + term
        for i in range(NV):
            x = pltpu.roll(tangent[i], 1, 1)
            x = jnp.where(lane == 0, pltpu.roll(x, 1, 0), x)
            out[i * OWN + t] = sums[i] - flow * x + mix[i * OWN + t]
            x = pltpu.roll(flow * dual[i], LANE - 1, 1)
            x = jnp.where(lane == LANE - 1, pltpu.roll(x, SUB - 1, 0), x)
            out[(NV + i) * OWN + t] = dsums[i] - x + mix[(NV + i) * OWN + t]
        return carry

    for n in range(CHUNKS):
        chunks[n].wait()
        load_blocks(j_v, m_s, CHUNK * n, CHUNK)
        lax.fori_loop(CHUNK * n, CHUNK * (n + 1), body, 0)


def final_kernel(
    partial, from_prev, from_next, m_s, up_weight, lo_weight, up_cells, lo_cells,
    tangent_out, adjoint_out, uw, lw, uc, lc, sems,
):
    for copy in fetch([(up_weight, uw), (lo_weight, lw), (up_cells, uc), (lo_cells, lc)], sems):
        copy.wait()
    lane = lanes()
    quarter = lane >> 5
    up_index = quarters(uc[...]) & (LANE - 1)
    lo_index = quarters(lc[...]) & (LANE - 1)
    up_hit = take(up_index, lane >> 2) == lane
    lo_hit = take(lo_index, lane >> 2) == lane
    up_scale = quarters(uw[...])
    lo_scale = quarters(lw[...])
    lo_mid = jnp.where(quarter == 0, lo_scale, 1.0)
    up_mid = jnp.where(quarter == 1, up_scale, 1.0)
    spots = [32 * g + (lane >> 2) for g in range(4)]

    def body(t, carry):
        prev = [from_prev[OWN * j + t] for j in range(3)]
        next_ = [from_next[OWN * j + t] for j in range(3)]
        prev = [prev[0] * lo_scale, prev[1] * lo_mid, prev[2]]
        next_ = [next_[0] * up_scale, next_[1] * up_mid, next_[2]]
        rows = []
        for q in range(2 * NV):
            low = take(prev[q // 4], spots[q % 4])
            high = take(next_[q // 4], spots[(q % 4) ^ 1])
            value = partial[q * OWN + t]
            value = value - jnp.where(lo_hit, low, 0.0)
            value = value - jnp.where(up_hit, high, 0.0)
            rows.append(value)
        for i in range(NV):
            total = block_row(m_s, t, i * NV) * rows[0]
            for j in range(1, NV):
                total = total + block_row(m_s, t, i * NV + j) * rows[j]
            tangent_out[i * OWN + t] = total
            adjoint_out[i * OWN + t] = rows[NV + i]
        return carry

    lax.fori_loop(0, OWN, body, 0)


def rows_of(count):
    return jax.ShapeDtypeStruct((count, SUB, LANE), jnp.float32)


BLOCK = (SUB * MPITCH, LANE)
BLOCKS = jax.ShapeDtypeStruct(BLOCK, jnp.float32)
ANY = pl.BlockSpec(memory_space=pl.ANY)
VMEM = pl.BlockSpec(memory_space=pltpu.VMEM)
SMEM = pl.BlockSpec(memory_space=pltpu.SMEM)


def held(shape, dtype=jnp.float32):
    return pltpu.VMEM(shape, dtype)


def sems(count):
    return pltpu.SemaphoreType.DMA((count,))


def call(kernel, in_specs, out_shape, scratch, name):
    return pl.pallas_call(
        kernel,
        in_specs=in_specs,
        out_shape=out_shape,
        scratch_shapes=scratch,
        compiler_params=pltpu.CompilerParams(vmem_limit_bytes=24 << 20),
        name=name,
    )


def on_device(
    tangent_seed,
    adjoint_seed,
    jacobian,
    precond,
    upwind,
    up_weight,
    bottom_face_strength,
    up_cells,
    lo_cells,
    phase_index,
):
    face = up_cells.shape[0]
    tables = (up_weight, bottom_face_strength, up_cells.reshape(1, face), lo_cells.reshape(1, face))
    table_scratch = [held((1, face)), held((1, face)), held((1, face), jnp.int32), held((1, face), jnp.int32)]
    rows = (ROWS, SUB, LANE)
    both = (2, FIELD, SUB, LANE)
    fields, precond_rows = call(
        dual_kernel,
        [ANY, ANY, ANY],
        (rows_of(FIELD), BLOCKS),
        [held(precond.shape, precond.dtype), held(rows), sems(2), sems(CHUNKS)],
        "dual",
    )(tangent_seed.reshape(rows), adjoint_seed.reshape(rows), precond)
    gathered = lax.all_gather(fields, "inst", axis=0, tiled=True).reshape(both)
    up_face, lo_face = call(
        rotate_kernel,
        [SMEM, ANY, ANY, ANY, ANY, ANY],
        (rows_of(FACE_ROWS), rows_of(FACE_ROWS)),
        [held(both), *table_scratch, held((SNAPS, SUB, LANE)), held((3, SNAPS, SUB, LANE)), held((3, SNAPS, SUB, LANE)), sems(5)],
        "rotate",
    )(phase_index, gathered, *tables)
    from_prev = passed_along(up_face, "blade", 1)
    from_next = passed_along(lo_face, "blade", -1)
    partial = call(
        local_kernel,
        [ANY, ANY, ANY],
        rows_of(FIELD),
        [held(both), held(jacobian.shape, jacobian.dtype), held(upwind.shape), held(BLOCK), held((FIELD, SUB, LANE)), sems(2), sems(CHUNKS)],
        "local",
    )(gathered, jacobian, upwind)
    tangent_out, adjoint_out = call(
        final_kernel,
        [VMEM, VMEM, VMEM, VMEM, ANY, ANY, ANY, ANY],
        (rows_of(ROWS), rows_of(ROWS)),
        [*table_scratch, sems(4)],
        "final",
    )(partial, from_prev, from_next, precond_rows, *tables)
    return tangent_out.reshape(tangent_seed.shape), adjoint_out.reshape(adjoint_seed.shape)


def solution(mesh):
    in_specs = (
        P("blade", None, "inst", None),
        P("blade", None, "inst", None),
        P("blade", "inst", None, None),
        P("blade", "inst", None, None),
        P("blade", None),
        P("blade", None),
        P("blade", None),
        P(),
        P(),
        P(),
    )
    out_specs = (P("blade", None, "inst", None), P("blade", None, "inst", None))
    return jax.shard_map(
        on_device, mesh=mesh, in_specs=in_specs, out_specs=out_specs, check_vma=False
    )
```

```python
import math

import jax
import jax.numpy as jnp
from jax import lax
from jax.experimental import pallas as pl
from jax.experimental.pallas import tpu as pltpu
from jax.sharding import PartitionSpec as P

SNAPS = 24
NH = 11
NV = 5
OWN = 12
OMEGA = 0.15
SUB, LANE = 8, 128
ROWS = NV * OWN
FIELD = 2 * ROWS
FACE_ROWS = 5 * OWN // 2
MPITCH = OWN * 32 + 8
CHUNKS = 2
CHUNK = OWN // CHUNKS
OUT_CHUNKS = 3
OUT_CHUNK = OWN // OUT_CHUNKS


def derivative_weights():
    weights = [0.0]
    for n in range(1, 12):
        total = sum(k * math.sin(2 * math.pi * ((k * n) % SNAPS) / SNAPS) for k in range(1, NH + 1))
        weights.append(-(2.0 / SNAPS) * total)
    return weights


DERIV = derivative_weights()


def exchanged(block, late):
    count, cores = lax.axis_size("blade"), lax.axis_size("inst")
    route = []
    for i in range(count):
        for core in range(cores):
            partner = (i + 1 if (i + core + late) % 2 == 1 else i - 1) % count
            route.append((i * cores + core, partner * cores + core))
    return lax.ppermute(block, ("blade", "inst"), route)


def first_face():
    return (lax.axis_index("blade") + lax.axis_index("inst") + 1) % 2


def lanes():
    return lax.broadcasted_iota(jnp.int32, (SUB, LANE), 1)


def sublanes():
    return lax.broadcasted_iota(jnp.int32, (SUB, LANE), 0)


def take(x, index):
    return jnp.take_along_axis(x, index, axis=1, mode="promise_in_bounds")


def quarters(row):
    first = jnp.broadcast_to(row[:, :LANE], (SUB, LANE))
    second = jnp.broadcast_to(row[:, LANE:], (SUB, LANE))
    sub = sublanes()
    both = jnp.where(sub < 4, first, second)
    return take(both, 32 * (sub & 3) + (lanes() & 31))


def wide(row):
    return jnp.concatenate([row[:, LANE * k : LANE * (k + 1)] for k in range(SUB)], axis=0)


def load_blocks(blocks, scratch, t):
    for k in range(SUB):
        tile = blocks[0, t, :, LANE * k : LANE * (k + 1)].astype(jnp.float32)
        scratch[pl.ds(pl.multiple_of(k * MPITCH + t * 32, 8), NV * NV), :] = tile


def fetch(pairs, sems):
    copies = [pltpu.make_async_copy(src, dst, sems.at[n]) for n, (src, dst) in enumerate(pairs)]
    for copy in copies:
        copy.start()
    return copies


def fetch_blocks(blocks, scratch, sems):
    return fetch(
        [(blocks.at[:, pl.ds(CHUNK * n, CHUNK)], scratch.at[:, pl.ds(CHUNK * n, CHUNK)]) for n in range(CHUNKS)],
        sems,
    )


def block_row(scratch, t, ij):
    return scratch[pl.ds(t * 32 + ij, SUB, stride=MPITCH), :]


def packed(parts, quarter):
    result = parts[-1]
    for g in reversed(range(len(parts) - 1)):
        result = jnp.where(quarter == g, parts[g], result)
    return result


def phase_weights(phase, rho):
    shape = (16, LANE)
    order = lax.broadcasted_iota(jnp.int32, shape, 0) + 1
    lag = lax.broadcasted_iota(jnp.int32, shape, 1)
    padded = jnp.concatenate([phase[...], jnp.zeros((1, LANE - NH), jnp.int32)], axis=1)
    spread = jnp.where(lag == order - 1, jnp.broadcast_to(padded, shape), 0).astype(jnp.float32)
    index = jnp.sum(spread, axis=1, keepdims=True)
    turns = (32 * order * (lag & 31)).astype(jnp.float32) - 3.0 * index
    turns = turns - 768.0 * jnp.floor(turns * (1.0 / 768.0) + 0.5)
    waves = jnp.where(order <= NH, jnp.cos(turns * (2.0 * math.pi / 768.0)), 0.0)
    parity = (1 - (lag[:1] & 1)).astype(jnp.float32)
    row = (2.0 / SNAPS) * (parity + jnp.sum(waves, axis=0, keepdims=True))
    for n in range(SNAPS):
        value = jnp.broadcast_to(row[:, n : n + 1], (SUB, LANE))
        rho[0, (-n) % SNAPS] = value
        rho[1, n] = value


def dual_kernel(
    phase, tangent, adjoint, precond, up_weight, lo_weight, up_cells, lo_cells,
    out, m_s, rho, index, scale, p_v, a_v, ph, uw, lw, uc, lc, t_sem, p_sem, w_sem,
):
    small = fetch(
        [(phase, ph), (up_weight, uw), (lo_weight, lw), (up_cells, uc), (lo_cells, lc)], w_sem
    )
    seeds = fetch([(adjoint, a_v), (tangent, out.at[pl.ds(0, ROWS)])], t_sem)
    chunks = fetch_blocks(precond, p_v, p_sem)
    for copy in small:
        copy.wait()
    phase_weights(ph, rho)
    index[0] = quarters(uc[...]) & (LANE - 1)
    index[1] = quarters(lc[...]) & (LANE - 1)
    up_scale = quarters(uw[...])
    lo_scale = quarters(lw[...])
    quarter = lanes() >> 5
    scale[0] = up_scale
    scale[1] = lo_scale
    scale[2] = jnp.where(quarter == 0, 1.0, up_scale)
    scale[3] = jnp.where(quarter == 1, 1.0, lo_scale)
    scale[4] = jnp.where(quarter == 0, lo_scale, 1.0)
    scale[5] = jnp.where(quarter == 1, up_scale, 1.0)

    def apply(t):
        seed = [a_v[i * OWN + t] for i in range(NV)]
        for j in range(NV):
            total = block_row(m_s, t, j) * seed[0]
            for i in range(1, NV):
                total = total + block_row(m_s, t, i * NV + j) * seed[i]
            out[ROWS + j * OWN + t] = total

    seeds[0].wait()
    for t in range(OWN):
        if t % CHUNK == 0:
            chunks[t // CHUNK].wait()
        load_blocks(p_v, m_s, t)
        if t > 0:
            apply(t - 1)
    apply(OWN - 1)
    seeds[1].wait()


def early():
    return lax.axis_index("blade") == 0


def local_work(gathered, jacobian, upwind, out, m_s, mix):
    own = lax.axis_index("inst")

    for fld, sign in ((0, 1.0), (1, -1.0)):

        def mix_body(i, carry):
            base = (fld * NV + i) * OWN
            mine = [gathered[own, base + s] for s in range(OWN)]
            theirs = [gathered[1 - own, base + s] for s in range(OWN)]
            ring = mine + theirs
            for r in range(OWN):
                total = None
                for k in range(1, OWN):
                    term = (sign * OMEGA * DERIV[k]) * (ring[(r - k) % SNAPS] - ring[(r + k) % SNAPS])
                    total = term if total is None else total + term
                mix[base + r] = total
            return carry

        lax.fori_loop(0, NV, mix_body, 0)

    lane = lanes()
    cell = sublanes() * LANE + lane
    flow = jnp.where(cell == 0, 0.0, wide(upwind[...]))

    def body(t, carry):
        tangent = [gathered[own, i * OWN + t] for i in range(NV)]
        dual = [gathered[own, (NV + i) * OWN + t] for i in range(NV)]
        sums = [None] * NV
        dsums = [None] * NV
        for i in range(NV):
            for j in range(NV):
                m = block_row(m_s, t, i * NV + j)
                term = m * tangent[j]
                sums[i] = term if j == 0 else sums[i] + term
                term = m * dual[i]
                dsums[j] = term if i == 0 else dsums[j] + term
        for i in range(NV):
            x = pltpu.roll(tangent[i], 1, 1)
            x = jnp.where(lane == 0, pltpu.roll(x, 1, 0), x)
            out[i * OWN + t] = sums[i] - flow * x + mix[i * OWN + t]
            x = pltpu.roll(flow * dual[i], LANE - 1, 1)
            x = jnp.where(lane == LANE - 1, pltpu.roll(x, SUB - 1, 0), x)
            out[(NV + i) * OWN + t] = dsums[i] - x + mix[(NV + i) * OWN + t]
        return carry

    def prepare(t, carry):
        load_blocks(jacobian, m_s, t)
        return carry

    lax.fori_loop(0, OWN, prepare, 0)
    lax.fori_loop(0, OWN, body, 0)


def local_kernel(gathered, jacobian, upwind, given, out, m_s, mix):
    @pl.when(jnp.logical_not(early()))
    def _():
        local_work(gathered, jacobian, upwind, out, m_s, mix)


def rotate_kernel(
    gathered, jacobian, upwind, rho, index, scale, ahead, after, partial, f_s, m_s, mix
):
    own = lax.axis_index("inst")
    first = first_face()
    quarter = lanes() >> 5
    odd = (quarter & 1) == 1
    even_rows = jnp.where(odd, index[1], index[0])
    odd_rows = jnp.where(odd, index[0], index[1])

    for n in range(SNAPS):
        core, t = (own, n) if n < OWN else (1 - own, n - OWN)
        rows = [
            take(gathered[core, q * OWN + t], odd_rows if q % 2 else even_rows)
            for q in range(2 * NV)
        ]
        for side in range(2):
            order = [rows[q ^ side] for q in range(2 * NV)]
            f_s[side, 0, n] = packed(order[:4], quarter)
            f_s[side, 1, n] = packed(order[4:8], quarter)
            f_s[side, 2, n] = jnp.where(odd, order[9], order[8])

    for result, which in ((ahead, first), (after, 1 - first)):
        for j in range(3):
            sums = [None] * OWN
            for s in range(SNAPS):
                x = f_s[which, j, s]
                for r in range(OWN):
                    term = rho[which, (r - s) % SNAPS] * x
                    sums[r] = term if sums[r] is None else sums[r] + term
            if j == 0:
                for r in range(OWN):
                    result[r] = sums[r]
            elif j == 1:
                for r in range(OWN):
                    result[OWN + r] = sums[r] * scale[2 + which]
            else:
                for r in range(OWN // 2):
                    both = jnp.where(quarter < 2, sums[r], sums[r + OWN // 2])
                    result[2 * OWN + r] = both * scale[which]

    @pl.when(early())
    def _():
        local_work(gathered, jacobian, upwind, partial, m_s, mix)


def final_kernel(
    partial, ahead, after, m_s, index, scale, tangent_out, adjoint_out, t_v, a_v, o_sem
):
    first = first_face()
    lane = lanes()
    group = lane >> 2
    faces = []
    for face, which in ((after, first), (ahead, 1 - first)):
        hit = take(index[1 - which], group) == lane
        spots = [group + 32 * (g + which * (1 - 2 * (g % 2))) for g in range(4)]
        faces.append((face, hit, spots, scale[1 - which], scale[4 + which]))

    def apply(t):
        half, low = divmod(t, OWN // 2)
        rows = [partial[q * OWN + t] for q in range(2 * NV)]
        for face, hit, spots, full, mid in faces:
            parts = [face[t] * full, face[OWN + t] * mid, face[2 * OWN + low]]
            for q in range(2 * NV):
                g = q % 4 + 2 * half if q >= 8 else q % 4
                rows[q] = rows[q] - jnp.where(hit, take(parts[q // 4], spots[g]), 0.0)
        for i in range(NV):
            total = block_row(m_s, t, i * NV) * rows[0]
            for j in range(1, NV):
                total = total + block_row(m_s, t, i * NV + j) * rows[j]
            t_v[i, t] = total
            a_v[i, t] = rows[NV + i]

    copies = []
    for n in range(OUT_CHUNKS):
        span = pl.ds(OUT_CHUNK * n, OUT_CHUNK)
        for t in range(OUT_CHUNK * n, OUT_CHUNK * (n + 1)):
            apply(t)
        for side, (src, dst) in enumerate(((t_v, tangent_out), (a_v, adjoint_out))):
            copy = pltpu.make_async_copy(src.at[:, span], dst.at[:, span], o_sem.at[2 * n + side])
            copy.start()
            copies.append(copy)
    for copy in copies:
        copy.wait()


def rows_of(count):
    return jax.ShapeDtypeStruct((count, SUB, LANE), jnp.float32)


BLOCK = (SUB * MPITCH, LANE)
BLOCKS = jax.ShapeDtypeStruct(BLOCK, jnp.float32)
HBM = pl.BlockSpec(memory_space=pltpu.HBM)
VMEM = pl.BlockSpec(memory_space=pltpu.VMEM)


def held(shape, dtype=jnp.float32):
    return pltpu.VMEM(shape, dtype)


def sems(count):
    return pltpu.SemaphoreType.DMA((count,))


def call(kernel, in_specs, out_shape, scratch, name, aliases={}, **kinds):
    return pl.pallas_call(
        kernel,
        in_specs=in_specs,
        out_shape=out_shape,
        scratch_shapes=scratch,
        input_output_aliases=aliases,
        compiler_params=pltpu.CompilerParams(vmem_limit_bytes=24 << 20),
        name=name,
        **kinds,
    )


def on_device(
    tangent_seed,
    adjoint_seed,
    jacobian,
    precond,
    upwind,
    up_weight,
    bottom_face_strength,
    up_cells,
    lo_cells,
    phase_index,
):
    face = up_cells.shape[0]
    tables = (phase_index.reshape(1, phase_index.shape[0]), up_weight, bottom_face_strength, up_cells.reshape(1, face), lo_cells.reshape(1, face))
    rows = (ROWS, SUB, LANE)
    both = (2, FIELD, SUB, LANE)
    fields, precond_rows, rho, index, scale = call(
        dual_kernel,
        [HBM] * 8,
        (
            rows_of(FIELD),
            BLOCKS,
            jax.ShapeDtypeStruct((2, SNAPS, SUB, LANE), jnp.float32),
            jax.ShapeDtypeStruct((2, SUB, LANE), jnp.int32),
            rows_of(6),
        ),
        [
            held(precond.shape, precond.dtype),
            held(rows),
            held(tables[0].shape, jnp.int32),
            held((1, face)),
            held((1, face)),
            held((1, face), jnp.int32),
            held((1, face), jnp.int32),
            sems(2),
            sems(CHUNKS),
            sems(5),
        ],
        "dual",
    )(
        *[
            pltpu.with_memory_space_constraint(x, pltpu.HBM)
            for x in (tables[0], tangent_seed.reshape(rows), adjoint_seed.reshape(rows), precond, *tables[1:])
        ],
    )
    gathered = lax.all_gather(fields, "inst", axis=0, tiled=True).reshape(both)
    local_scratch = [held(BLOCK), held((FIELD, SUB, LANE))]
    ahead, after, partial = call(
        rotate_kernel,
        [VMEM] * 6,
        (rows_of(FACE_ROWS), rows_of(FACE_ROWS), rows_of(FIELD)),
        [held((2, 3, SNAPS, SUB, LANE)), *local_scratch],
        "rotate",
    )(gathered, jacobian, upwind, rho, index, scale)
    ahead = exchanged(ahead, 0)
    after = exchanged(after, 1)
    partial = call(
        local_kernel, [VMEM] * 4, rows_of(FIELD), local_scratch, "local", {3: 0}
    )(gathered, jacobian, upwind, partial)
    out = (NV, OWN, SUB, LANE)
    tangent_out, adjoint_out = call(
        final_kernel,
        [VMEM] * 6,
        (jax.ShapeDtypeStruct(out, jnp.float32), jax.ShapeDtypeStruct(out, jnp.float32)),
        [held(out), held(out), sems(2 * OUT_CHUNKS)],
        "final",
        out_specs=(HBM, HBM),
    )(partial, ahead, after, precond_rows, index, scale)
    return tangent_out.reshape(tangent_seed.shape), adjoint_out.reshape(adjoint_seed.shape)


def solution(mesh):
    in_specs = (
        P("blade", None, "inst", None),
        P("blade", None, "inst", None),
        P("blade", "inst", None, None),
        P("blade", "inst", None, None),
        P("blade", None),
        P("blade", None),
        P("blade", None),
        P(),
        P(),
        P(),
    )
    out_specs = (P("blade", None, "inst", None), P("blade", None, "inst", None))
    return jax.shard_map(
        on_device, mesh=mesh, in_specs=in_specs, out_specs=out_specs, check_vma=False
    )
```

```python
import math

import jax
import jax.numpy as jnp
from jax import lax
from jax.experimental import pallas as pl
from jax.experimental.pallas import tpu as pltpu
from jax.sharding import PartitionSpec as P

SNAPS = 24
NH = 11
NV = 5
OWN = 12
OMEGA = 0.15
SUB, LANE = 8, 128
ROWS = NV * OWN
FIELD = 2 * ROWS
FACE_ROWS = 5 * OWN // 2
MPITCH = OWN * 32 + 8
CHUNKS = 2
CHUNK = OWN // CHUNKS
OUT_CHUNKS = 3
OUT_CHUNK = OWN // OUT_CHUNKS


def derivative_weights():
    weights = [0.0]
    for n in range(1, 12):
        total = sum(k * math.sin(2 * math.pi * ((k * n) % SNAPS) / SNAPS) for k in range(1, NH + 1))
        weights.append(-(2.0 / SNAPS) * total)
    return weights


DERIV = derivative_weights()


def exchanged(block, late):
    count, cores = lax.axis_size("blade"), lax.axis_size("inst")
    route = []
    for i in range(count):
        for core in range(cores):
            partner = (i + 1 if (i + core + late) % 2 == 1 else i - 1) % count
            route.append((i * cores + core, partner * cores + core))
    return lax.ppermute(block, ("blade", "inst"), route)


def first_face():
    return (lax.axis_index("blade") + lax.axis_index("inst") + 1) % 2


def lanes():
    return lax.broadcasted_iota(jnp.int32, (SUB, LANE), 1)


def sublanes():
    return lax.broadcasted_iota(jnp.int32, (SUB, LANE), 0)


def take(x, index):
    return jnp.take_along_axis(x, index, axis=1, mode="promise_in_bounds")


def quarters(row):
    first = jnp.broadcast_to(row[:, :LANE], (SUB, LANE))
    second = jnp.broadcast_to(row[:, LANE:], (SUB, LANE))
    sub = sublanes()
    both = jnp.where(sub < 4, first, second)
    return take(both, 32 * (sub & 3) + (lanes() & 31))


def wide(row):
    return jnp.concatenate([row[:, LANE * k : LANE * (k + 1)] for k in range(SUB)], axis=0)


def load_blocks(blocks, scratch, t):
    for k in range(SUB):
        tile = blocks[0, t, :, LANE * k : LANE * (k + 1)].astype(jnp.float32)
        scratch[pl.ds(pl.multiple_of(k * MPITCH + t * 32, 8), NV * NV), :] = tile


def fetch(pairs, sems):
    copies = [pltpu.make_async_copy(src, dst, sems.at[n]) for n, (src, dst) in enumerate(pairs)]
    for copy in copies:
        copy.start()
    return copies


def fetch_blocks(blocks, scratch, sems):
    return fetch(
        [(blocks.at[:, pl.ds(CHUNK * n, CHUNK)], scratch.at[:, pl.ds(CHUNK * n, CHUNK)]) for n in range(CHUNKS)],
        sems,
    )


def block_row(scratch, t, ij):
    return scratch[pl.ds(t * 32 + ij, SUB, stride=MPITCH), :]


def packed(parts, quarter):
    result = parts[-1]
    for g in reversed(range(len(parts) - 1)):
        result = jnp.where(quarter == g, parts[g], result)
    return result


def phase_weights(phase, rho):
    shape = (16, LANE)
    order = lax.broadcasted_iota(jnp.int32, shape, 0) + 1
    lag = lax.broadcasted_iota(jnp.int32, shape, 1)
    padded = jnp.concatenate([phase[...], jnp.zeros((1, LANE - NH), jnp.int32)], axis=1)
    spread = jnp.where(lag == order - 1, jnp.broadcast_to(padded, shape), 0).astype(jnp.float32)
    index = jnp.sum(spread, axis=1, keepdims=True)
    turns = (32 * order * (lag & 31)).astype(jnp.float32) - 3.0 * index
    turns = turns - 768.0 * jnp.floor(turns * (1.0 / 768.0) + 0.5)
    waves = jnp.where(order <= NH, jnp.cos(turns * (2.0 * math.pi / 768.0)), 0.0)
    parity = (1 - (lag[:1] & 1)).astype(jnp.float32)
    row = (2.0 / SNAPS) * (parity + jnp.sum(waves, axis=0, keepdims=True))
    for n in range(SNAPS):
        value = jnp.broadcast_to(row[:, n : n + 1], (SUB, LANE))
        rho[0, (-n) % SNAPS] = value
        rho[1, n] = value


def dual_kernel(
    phase, tangent, adjoint, precond, up_weight, lo_weight, up_cells, lo_cells,
    out, m_s, rho, index, scale, p_v, a_v, ph, uw, lw, uc, lc, t_sem, p_sem, w_sem,
):
    small = fetch(
        [(phase, ph), (up_weight, uw), (lo_weight, lw), (up_cells, uc), (lo_cells, lc)], w_sem
    )
    seeds = fetch([(adjoint, a_v), (tangent, out.at[pl.ds(0, ROWS)])], t_sem)
    chunks = fetch_blocks(precond, p_v, p_sem)
    for copy in small:
        copy.wait()
    phase_weights(ph, rho)
    index[0] = quarters(uc[...]) & (LANE - 1)
    index[1] = quarters(lc[...]) & (LANE - 1)
    up_scale = quarters(uw[...])
    lo_scale = quarters(lw[...])
    quarter = lanes() >> 5
    scale[0] = up_scale
    scale[1] = lo_scale
    scale[2] = jnp.where(quarter == 0, 1.0, up_scale)
    scale[3] = jnp.where(quarter == 1, 1.0, lo_scale)
    scale[4] = jnp.where(quarter == 0, lo_scale, 1.0)
    scale[5] = jnp.where(quarter == 1, up_scale, 1.0)

    def apply(t):
        seed = [a_v[i * OWN + t] for i in range(NV)]
        for j in range(NV):
            total = block_row(m_s, t, j) * seed[0]
            for i in range(1, NV):
                total = total + block_row(m_s, t, i * NV + j) * seed[i]
            out[ROWS + j * OWN + t] = total

    seeds[0].wait()
    for t in range(OWN):
        if t % CHUNK == 0:
            chunks[t // CHUNK].wait()
        load_blocks(p_v, m_s, t)
        if t > 0:
            apply(t - 1)
    apply(OWN - 1)
    seeds[1].wait()


def early():
    return lax.axis_index("blade") == 0


def local_work(gathered, jacobian, upwind, out, m_s, mix):
    own = lax.axis_index("inst")

    for fld, sign in ((0, 1.0), (1, -1.0)):

        def mix_body(i, carry):
            base = (fld * NV + i) * OWN
            mine = [gathered[own, base + s] for s in range(OWN)]
            theirs = [gathered[1 - own, base + s] for s in range(OWN)]
            ring = mine + theirs
            for r in range(OWN):
                total = None
                for k in range(1, OWN):
                    term = (sign * OMEGA * DERIV[k]) * (ring[(r - k) % SNAPS] - ring[(r + k) % SNAPS])
                    total = term if total is None else total + term
                mix[base + r] = total
            return carry

        lax.fori_loop(0, NV, mix_body, 0)

    lane = lanes()
    cell = sublanes() * LANE + lane
    flow = jnp.where(cell == 0, 0.0, wide(upwind[...]))

    def body(t, carry):
        tangent = [gathered[own, i * OWN + t] for i in range(NV)]
        dual = [gathered[own, (NV + i) * OWN + t] for i in range(NV)]
        sums = [None] * NV
        dsums = [None] * NV
        for i in range(NV):
            for j in range(NV):
                m = block_row(m_s, t, i * NV + j)
                term = m * tangent[j]
                sums[i] = term if j == 0 else sums[i] + term
                term = m * dual[i]
                dsums[j] = term if i == 0 else dsums[j] + term
        for i in range(NV):
            x = pltpu.roll(tangent[i], 1, 1)
            x = jnp.where(lane == 0, pltpu.roll(x, 1, 0), x)
            out[i * OWN + t] = sums[i] - flow * x + mix[i * OWN + t]
            x = pltpu.roll(flow * dual[i], LANE - 1, 1)
            x = jnp.where(lane == LANE - 1, pltpu.roll(x, SUB - 1, 0), x)
            out[(NV + i) * OWN + t] = dsums[i] - x + mix[(NV + i) * OWN + t]
        return carry

    def prepare(t, carry):
        load_blocks(jacobian, m_s, t)
        return carry

    lax.fori_loop(0, OWN, prepare, 0)
    lax.fori_loop(0, OWN, body, 0)


def received(face, which, index, scale):
    lane = lanes()
    group = lane >> 2
    hit = take(index[1 - which], group) == lane
    spots = [group + 32 * (g + which * (1 - 2 * (g % 2))) for g in range(4)]
    full, mid = scale[1 - which], scale[4 + which]

    def terms(t):
        half, low = divmod(t, OWN // 2)
        parts = [face[t] * full, face[OWN + t] * mid, face[2 * OWN + low]]
        return [
            jnp.where(hit, take(parts[q // 4], spots[q % 4 + (2 * half if q >= 8 else 0)]), 0.0)
            for q in range(2 * NV)
        ]

    return terms


def local_kernel(gathered, jacobian, upwind, given, ahead, index, scale, out, m_s, mix):
    @pl.when(jnp.logical_not(early()))
    def _():
        local_work(gathered, jacobian, upwind, out, m_s, mix)

    terms = received(ahead, 1 - first_face(), index, scale)
    for t in range(OWN):
        for q, term in enumerate(terms(t)):
            out[q * OWN + t] = out[q * OWN + t] - term


def rotate_kernel(
    gathered, jacobian, upwind, rho, index, scale, ahead, after, partial, f_s, m_s, mix
):
    own = lax.axis_index("inst")
    first = first_face()
    quarter = lanes() >> 5
    odd = (quarter & 1) == 1
    even_rows = jnp.where(odd, index[1], index[0])
    odd_rows = jnp.where(odd, index[0], index[1])

    for n in range(SNAPS):
        core, t = (own, n) if n < OWN else (1 - own, n - OWN)
        rows = [
            take(gathered[core, q * OWN + t], odd_rows if q % 2 else even_rows)
            for q in range(2 * NV)
        ]
        for side in range(2):
            order = [rows[q ^ side] for q in range(2 * NV)]
            f_s[side, 0, n] = packed(order[:4], quarter)
            f_s[side, 1, n] = packed(order[4:8], quarter)
            f_s[side, 2, n] = jnp.where(odd, order[9], order[8])

    for result, which in ((ahead, first), (after, 1 - first)):
        for j in range(3):
            sums = [None] * OWN
            for s in range(SNAPS):
                x = f_s[which, j, s]
                for r in range(OWN):
                    term = rho[which, (r - s) % SNAPS] * x
                    sums[r] = term if sums[r] is None else sums[r] + term
            if j == 0:
                for r in range(OWN):
                    result[r] = sums[r]
            elif j == 1:
                for r in range(OWN):
                    result[OWN + r] = sums[r] * scale[2 + which]
            else:
                for r in range(OWN // 2):
                    both = jnp.where(quarter < 2, sums[r], sums[r + OWN // 2])
                    result[2 * OWN + r] = both * scale[which]

    @pl.when(early())
    def _():
        local_work(gathered, jacobian, upwind, partial, m_s, mix)


def final_kernel(
    partial, after, m_s, index, scale, tangent_out, adjoint_out, t_v, a_v, o_sem
):
    terms = received(after, first_face(), index, scale)

    def apply(t):
        rows = [partial[q * OWN + t] - term for q, term in enumerate(terms(t))]
        for i in range(NV):
            total = block_row(m_s, t, i * NV) * rows[0]
            for j in range(1, NV):
                total = total + block_row(m_s, t, i * NV + j) * rows[j]
            t_v[i, t] = total
            a_v[i, t] = rows[NV + i]

    copies = []
    for n in range(OUT_CHUNKS):
        span = pl.ds(OUT_CHUNK * n, OUT_CHUNK)
        for t in range(OUT_CHUNK * n, OUT_CHUNK * (n + 1)):
            apply(t)
        for side, (src, dst) in enumerate(((t_v, tangent_out), (a_v, adjoint_out))):
            copy = pltpu.make_async_copy(src.at[:, span], dst.at[:, span], o_sem.at[2 * n + side])
            copy.start()
            copies.append(copy)
    for copy in copies:
        copy.wait()


def rows_of(count):
    return jax.ShapeDtypeStruct((count, SUB, LANE), jnp.float32)


BLOCK = (SUB * MPITCH, LANE)
BLOCKS = jax.ShapeDtypeStruct(BLOCK, jnp.float32)
HBM = pl.BlockSpec(memory_space=pltpu.HBM)
VMEM = pl.BlockSpec(memory_space=pltpu.VMEM)


def held(shape, dtype=jnp.float32):
    return pltpu.VMEM(shape, dtype)


def sems(count):
    return pltpu.SemaphoreType.DMA((count,))


def call(kernel, in_specs, out_shape, scratch, name, aliases={}, **kinds):
    return pl.pallas_call(
        kernel,
        in_specs=in_specs,
        out_shape=out_shape,
        scratch_shapes=scratch,
        input_output_aliases=aliases,
        compiler_params=pltpu.CompilerParams(vmem_limit_bytes=24 << 20),
        name=name,
        **kinds,
    )


def on_device(
    tangent_seed,
    adjoint_seed,
    jacobian,
    precond,
    upwind,
    up_weight,
    bottom_face_strength,
    up_cells,
    lo_cells,
    phase_index,
):
    face = up_cells.shape[0]
    tables = (phase_index.reshape(1, phase_index.shape[0]), up_weight, bottom_face_strength, up_cells.reshape(1, face), lo_cells.reshape(1, face))
    rows = (ROWS, SUB, LANE)
    both = (2, FIELD, SUB, LANE)
    fields, precond_rows, rho, index, scale = call(
        dual_kernel,
        [HBM] * 8,
        (
            rows_of(FIELD),
            BLOCKS,
            jax.ShapeDtypeStruct((2, SNAPS, SUB, LANE), jnp.float32),
            jax.ShapeDtypeStruct((2, SUB, LANE), jnp.int32),
            rows_of(6),
        ),
        [
            held(precond.shape, precond.dtype),
            held(rows),
            held(tables[0].shape, jnp.int32),
            held((1, face)),
            held((1, face)),
            held((1, face), jnp.int32),
            held((1, face), jnp.int32),
            sems(2),
            sems(CHUNKS),
            sems(5),
        ],
        "dual",
    )(
        *[
            pltpu.with_memory_space_constraint(x, pltpu.HBM)
            for x in (tables[0], tangent_seed.reshape(rows), adjoint_seed.reshape(rows), precond, *tables[1:])
        ],
    )
    gathered = lax.all_gather(fields, "inst", axis=0, tiled=True).reshape(both)
    local_scratch = [held(BLOCK), held((FIELD, SUB, LANE))]
    ahead, after, partial = call(
        rotate_kernel,
        [VMEM] * 6,
        (rows_of(FACE_ROWS), rows_of(FACE_ROWS), rows_of(FIELD)),
        [held((2, 3, SNAPS, SUB, LANE)), *local_scratch],
        "rotate",
    )(gathered, jacobian, upwind, rho, index, scale)
    ahead = exchanged(ahead, 0)
    after = exchanged(after, 1)
    partial = call(
        local_kernel, [VMEM] * 7, rows_of(FIELD), local_scratch, "local", {3: 0}
    )(gathered, jacobian, upwind, partial, ahead, index, scale)
    out = (NV, OWN, SUB, LANE)
    tangent_out, adjoint_out = call(
        final_kernel,
        [VMEM] * 5,
        (jax.ShapeDtypeStruct(out, jnp.float32), jax.ShapeDtypeStruct(out, jnp.float32)),
        [held(out), held(out), sems(2 * OUT_CHUNKS)],
        "final",
        out_specs=(HBM, HBM),
    )(partial, after, precond_rows, index, scale)
    return tangent_out.reshape(tangent_seed.shape), adjoint_out.reshape(adjoint_seed.shape)


def solution(mesh):
    in_specs = (
        P("blade", None, "inst", None),
        P("blade", None, "inst", None),
        P("blade", "inst", None, None),
        P("blade", "inst", None, None),
        P("blade", None),
        P("blade", None),
        P("blade", None),
        P(),
        P(),
        P(),
    )
    out_specs = (P("blade", None, "inst", None), P("blade", None, "inst", None))
    return jax.shard_map(
        on_device, mesh=mesh, in_specs=in_specs, out_specs=out_specs, check_vma=False
    )
```

```python
import math

import jax
import jax.numpy as jnp
from jax import lax
from jax.experimental import pallas as pl
from jax.experimental.pallas import tpu as pltpu
from jax.sharding import PartitionSpec as P

SNAPS = 24
NH = 11
NV = 5
OWN = 12
OMEGA = 0.15
SUB, LANE = 8, 128
ROWS = NV * OWN
FIELD = 2 * ROWS
FACE_ROWS = 5 * OWN // 2
MPITCH = OWN * 32 + 8
CHUNKS = 2
CHUNK = OWN // CHUNKS
OUT_CHUNKS = 3
OUT_CHUNK = OWN // OUT_CHUNKS


def derivative_weights():
    weights = [0.0]
    for n in range(1, 12):
        total = sum(k * math.sin(2 * math.pi * ((k * n) % SNAPS) / SNAPS) for k in range(1, NH + 1))
        weights.append(-(2.0 / SNAPS) * total)
    return weights


DERIV = derivative_weights()


def exchanged(block, late):
    count, cores = lax.axis_size("blade"), lax.axis_size("inst")
    route = []
    for i in range(count):
        for core in range(cores):
            partner = (i + 1 if (i + core + late) % 2 == 1 else i - 1) % count
            route.append((i * cores + core, partner * cores + core))
    return lax.ppermute(block, ("blade", "inst"), route)


def first_face():
    return (lax.axis_index("blade") + lax.axis_index("inst") + 1) % 2


def lanes():
    return lax.broadcasted_iota(jnp.int32, (SUB, LANE), 1)


def sublanes():
    return lax.broadcasted_iota(jnp.int32, (SUB, LANE), 0)


def take(x, index):
    return jnp.take_along_axis(x, index, axis=1, mode="promise_in_bounds")


def quarters(row):
    first = jnp.broadcast_to(row[:, :LANE], (SUB, LANE))
    second = jnp.broadcast_to(row[:, LANE:], (SUB, LANE))
    sub = sublanes()
    both = jnp.where(sub < 4, first, second)
    return take(both, 32 * (sub & 3) + (lanes() & 31))


def wide(row):
    return jnp.concatenate([row[:, LANE * k : LANE * (k + 1)] for k in range(SUB)], axis=0)


def load_blocks(blocks, scratch, t):
    for k in range(SUB):
        tile = blocks[0, t, :, LANE * k : LANE * (k + 1)].astype(jnp.float32)
        scratch[pl.ds(pl.multiple_of(k * MPITCH + t * 32, 8), NV * NV), :] = tile


def fetch(pairs, sems):
    copies = [pltpu.make_async_copy(src, dst, sems.at[n]) for n, (src, dst) in enumerate(pairs)]
    for copy in copies:
        copy.start()
    return copies


def fetch_blocks(blocks, scratch, sems):
    return fetch(
        [(blocks.at[:, pl.ds(CHUNK * n, CHUNK)], scratch.at[:, pl.ds(CHUNK * n, CHUNK)]) for n in range(CHUNKS)],
        sems,
    )


def block_row(scratch, t, ij):
    return scratch[pl.ds(t * 32 + ij, SUB, stride=MPITCH), :]


def packed(parts, quarter):
    result = parts[-1]
    for g in reversed(range(len(parts) - 1)):
        result = jnp.where(quarter == g, parts[g], result)
    return result


def phase_weights(phase, rho):
    shape = (16, LANE)
    order = lax.broadcasted_iota(jnp.int32, shape, 0) + 1
    lag = lax.broadcasted_iota(jnp.int32, shape, 1)
    padded = jnp.concatenate([phase[...], jnp.zeros((1, LANE - NH), jnp.int32)], axis=1)
    spread = jnp.where(lag == order - 1, jnp.broadcast_to(padded, shape), 0).astype(jnp.float32)
    index = jnp.sum(spread, axis=1, keepdims=True)
    turns = (32 * order * (lag & 31)).astype(jnp.float32) - 3.0 * index
    turns = turns - 768.0 * jnp.floor(turns * (1.0 / 768.0) + 0.5)
    waves = jnp.where(order <= NH, jnp.cos(turns * (2.0 * math.pi / 768.0)), 0.0)
    parity = (1 - (lag[:1] & 1)).astype(jnp.float32)
    row = (2.0 / SNAPS) * (parity + jnp.sum(waves, axis=0, keepdims=True))
    for n in range(SNAPS):
        value = jnp.broadcast_to(row[:, n : n + 1], (SUB, LANE))
        rho[0, (-n) % SNAPS] = value
        rho[1, n] = value


def dual_kernel(
    phase, tangent, adjoint, precond, up_weight, lo_weight, up_cells, lo_cells,
    out, m_s, rho, index, scale, p_v, a_v, ph, uw, lw, uc, lc, t_sem, p_sem, w_sem,
):
    small = fetch(
        [(phase, ph), (up_weight, uw), (lo_weight, lw), (up_cells, uc), (lo_cells, lc)], w_sem
    )
    seeds = fetch([(adjoint, a_v), (tangent, out.at[pl.ds(0, ROWS)])], t_sem)
    chunks = fetch_blocks(precond, p_v, p_sem)
    for copy in small:
        copy.wait()
    phase_weights(ph, rho)
    index[0] = quarters(uc[...]) & (LANE - 1)
    index[1] = quarters(lc[...]) & (LANE - 1)
    up_scale = quarters(uw[...])
    lo_scale = quarters(lw[...])
    quarter = lanes() >> 5
    scale[0] = up_scale
    scale[1] = lo_scale
    scale[2] = jnp.where(quarter == 0, 1.0, up_scale)
    scale[3] = jnp.where(quarter == 1, 1.0, lo_scale)
    scale[4] = jnp.where(quarter == 0, lo_scale, 1.0)
    scale[5] = jnp.where(quarter == 1, up_scale, 1.0)

    def apply(t):
        seed = [a_v[i * OWN + t] for i in range(NV)]
        for j in range(NV):
            total = block_row(m_s, t, j) * seed[0]
            for i in range(1, NV):
                total = total + block_row(m_s, t, i * NV + j) * seed[i]
            out[ROWS + j * OWN + t] = total

    seeds[0].wait()
    for t in range(OWN):
        if t % CHUNK == 0:
            chunks[t // CHUNK].wait()
        load_blocks(p_v, m_s, t)
        if t > 0:
            apply(t - 1)
    apply(OWN - 1)
    seeds[1].wait()


def early():
    return lax.axis_index("blade") < 2


def local_work(gathered, jacobian, upwind, out, m_s, mix):
    own = lax.axis_index("inst")

    for fld, sign in ((0, 1.0), (1, -1.0)):

        def mix_body(i, carry):
            base = (fld * NV + i) * OWN
            mine = [gathered[own, base + s] for s in range(OWN)]
            theirs = [gathered[1 - own, base + s] for s in range(OWN)]
            ring = mine + theirs
            for r in range(OWN):
                total = None
                for k in range(1, OWN):
                    term = (sign * OMEGA * DERIV[k]) * (ring[(r - k) % SNAPS] - ring[(r + k) % SNAPS])
                    total = term if total is None else total + term
                mix[base + r] = total
            return carry

        lax.fori_loop(0, NV, mix_body, 0)

    lane = lanes()
    cell = sublanes() * LANE + lane
    flow = jnp.where(cell == 0, 0.0, wide(upwind[...]))

    def body(t, carry):
        tangent = [gathered[own, i * OWN + t] for i in range(NV)]
        dual = [gathered[own, (NV + i) * OWN + t] for i in range(NV)]
        sums = [None] * NV
        dsums = [None] * NV
        for i in range(NV):
            for j in range(NV):
                m = block_row(m_s, t, i * NV + j)
                term = m * tangent[j]
                sums[i] = term if j == 0 else sums[i] + term
                term = m * dual[i]
                dsums[j] = term if i == 0 else dsums[j] + term
        for i in range(NV):
            x = pltpu.roll(tangent[i], 1, 1)
            x = jnp.where(lane == 0, pltpu.roll(x, 1, 0), x)
            out[i * OWN + t] = sums[i] - flow * x + mix[i * OWN + t]
            x = pltpu.roll(flow * dual[i], LANE - 1, 1)
            x = jnp.where(lane == LANE - 1, pltpu.roll(x, SUB - 1, 0), x)
            out[(NV + i) * OWN + t] = dsums[i] - x + mix[(NV + i) * OWN + t]
        return carry

    def prepare(t, carry):
        load_blocks(jacobian, m_s, t)
        return carry

    lax.fori_loop(0, OWN, prepare, 0)
    lax.fori_loop(0, OWN, body, 0)


def received(face, which, index, scale):
    lane = lanes()
    group = lane >> 2
    hit = take(index[1 - which], group) == lane
    spots = [group + 32 * (g + which * (1 - 2 * (g % 2))) for g in range(4)]
    full, mid = scale[1 - which], scale[4 + which]

    def terms(t):
        half, low = divmod(t, OWN // 2)
        parts = [face[t] * full, face[OWN + t] * mid, face[2 * OWN + low]]
        return [
            jnp.where(hit, take(parts[q // 4], spots[q % 4 + (2 * half if q >= 8 else 0)]), 0.0)
            for q in range(2 * NV)
        ]

    return terms


def local_kernel(gathered, jacobian, upwind, given, ahead, index, scale, out, m_s, mix):
    @pl.when(jnp.logical_not(early()))
    def _():
        local_work(gathered, jacobian, upwind, out, m_s, mix)

    terms = received(ahead, 1 - first_face(), index, scale)
    for t in range(OWN):
        for q, term in enumerate(terms(t)):
            out[q * OWN + t] = out[q * OWN + t] - term


def rotate_kernel(
    gathered, jacobian, upwind, rho, index, scale, ahead, after, partial, f_s, m_s, mix
):
    own = lax.axis_index("inst")
    first = first_face()
    quarter = lanes() >> 5
    odd = (quarter & 1) == 1
    even_rows = jnp.where(odd, index[1], index[0])
    odd_rows = jnp.where(odd, index[0], index[1])

    for n in range(SNAPS):
        core, t = (own, n) if n < OWN else (1 - own, n - OWN)
        rows = [
            take(gathered[core, q * OWN + t], odd_rows if q % 2 else even_rows)
            for q in range(2 * NV)
        ]
        for side in range(2):
            order = [rows[q ^ side] for q in range(2 * NV)]
            f_s[side, 0, n] = packed(order[:4], quarter)
            f_s[side, 1, n] = packed(order[4:8], quarter)
            f_s[side, 2, n] = jnp.where(odd, order[9], order[8])

    for result, which in ((ahead, first), (after, 1 - first)):
        for j in range(3):
            sums = [None] * OWN
            for s in range(SNAPS):
                x = f_s[which, j, s]
                for r in range(OWN):
                    term = rho[which, (r - s) % SNAPS] * x
                    sums[r] = term if sums[r] is None else sums[r] + term
            if j == 0:
                for r in range(OWN):
                    result[r] = sums[r]
            elif j == 1:
                for r in range(OWN):
                    result[OWN + r] = sums[r] * scale[2 + which]
            else:
                for r in range(OWN // 2):
                    both = jnp.where(quarter < 2, sums[r], sums[r + OWN // 2])
                    result[2 * OWN + r] = both * scale[which]

    @pl.when(early())
    def _():
        local_work(gathered, jacobian, upwind, partial, m_s, mix)


def final_kernel(
    partial, after, m_s, index, scale, tangent_out, adjoint_out, t_v, a_v, o_sem
):
    terms = received(after, first_face(), index, scale)

    def apply(t):
        rows = [partial[q * OWN + t] - term for q, term in enumerate(terms(t))]
        for i in range(NV):
            total = block_row(m_s, t, i * NV) * rows[0]
            for j in range(1, NV):
                total = total + block_row(m_s, t, i * NV + j) * rows[j]
            t_v[i, t] = total
            a_v[i, t] = rows[NV + i]

    copies = []
    for n in range(OUT_CHUNKS):
        span = pl.ds(OUT_CHUNK * n, OUT_CHUNK)
        for t in range(OUT_CHUNK * n, OUT_CHUNK * (n + 1)):
            apply(t)
        for side, (src, dst) in enumerate(((t_v, tangent_out), (a_v, adjoint_out))):
            copy = pltpu.make_async_copy(src.at[:, span], dst.at[:, span], o_sem.at[2 * n + side])
            copy.start()
            copies.append(copy)
    for copy in copies:
        copy.wait()


def rows_of(count):
    return jax.ShapeDtypeStruct((count, SUB, LANE), jnp.float32)


BLOCK = (SUB * MPITCH, LANE)
BLOCKS = jax.ShapeDtypeStruct(BLOCK, jnp.float32)
HBM = pl.BlockSpec(memory_space=pltpu.HBM)
VMEM = pl.BlockSpec(memory_space=pltpu.VMEM)


def held(shape, dtype=jnp.float32):
    return pltpu.VMEM(shape, dtype)


def sems(count):
    return pltpu.SemaphoreType.DMA((count,))


def call(kernel, in_specs, out_shape, scratch, name, aliases={}, **kinds):
    return pl.pallas_call(
        kernel,
        in_specs=in_specs,
        out_shape=out_shape,
        scratch_shapes=scratch,
        input_output_aliases=aliases,
        compiler_params=pltpu.CompilerParams(vmem_limit_bytes=24 << 20),
        name=name,
        **kinds,
    )


def on_device(
    tangent_seed,
    adjoint_seed,
    jacobian,
    precond,
    upwind,
    up_weight,
    bottom_face_strength,
    up_cells,
    lo_cells,
    phase_index,
):
    face = up_cells.shape[0]
    tables = (phase_index.reshape(1, phase_index.shape[0]), up_weight, bottom_face_strength, up_cells.reshape(1, face), lo_cells.reshape(1, face))
    rows = (ROWS, SUB, LANE)
    both = (2, FIELD, SUB, LANE)
    fields, precond_rows, rho, index, scale = call(
        dual_kernel,
        [HBM] * 8,
        (
            rows_of(FIELD),
            BLOCKS,
            jax.ShapeDtypeStruct((2, SNAPS, SUB, LANE), jnp.float32),
            jax.ShapeDtypeStruct((2, SUB, LANE), jnp.int32),
            rows_of(6),
        ),
        [
            held(precond.shape, precond.dtype),
            held(rows),
            held(tables[0].shape, jnp.int32),
            held((1, face)),
            held((1, face)),
            held((1, face), jnp.int32),
            held((1, face), jnp.int32),
            sems(2),
            sems(CHUNKS),
            sems(5),
        ],
        "dual",
    )(
        *[
            pltpu.with_memory_space_constraint(x, pltpu.HBM)
            for x in (tables[0], tangent_seed.reshape(rows), adjoint_seed.reshape(rows), precond, *tables[1:])
        ],
    )
    gathered = lax.all_gather(fields, "inst", axis=0, tiled=True).reshape(both)
    local_scratch = [held(BLOCK), held((FIELD, SUB, LANE))]
    ahead, after, partial = call(
        rotate_kernel,
        [VMEM] * 6,
        (rows_of(FACE_ROWS), rows_of(FACE_ROWS), rows_of(FIELD)),
        [held((2, 3, SNAPS, SUB, LANE)), *local_scratch],
        "rotate",
    )(gathered, jacobian, upwind, rho, index, scale)
    ahead = exchanged(ahead, 0)
    after = exchanged(after, 1)
    partial = call(
        local_kernel, [VMEM] * 7, rows_of(FIELD), local_scratch, "local", {3: 0}
    )(gathered, jacobian, upwind, partial, ahead, index, scale)
    out = (NV, OWN, SUB, LANE)
    tangent_out, adjoint_out = call(
        final_kernel,
        [VMEM] * 5,
        (jax.ShapeDtypeStruct(out, jnp.float32), jax.ShapeDtypeStruct(out, jnp.float32)),
        [held(out), held(out), sems(2 * OUT_CHUNKS)],
        "final",
        out_specs=(HBM, HBM),
    )(partial, after, precond_rows, index, scale)
    return tangent_out.reshape(tangent_seed.shape), adjoint_out.reshape(adjoint_seed.shape)


def solution(mesh):
    in_specs = (
        P("blade", None, "inst", None),
        P("blade", None, "inst", None),
        P("blade", "inst", None, None),
        P("blade", "inst", None, None),
        P("blade", None),
        P("blade", None),
        P("blade", None),
        P(),
        P(),
        P(),
    )
    out_specs = (P("blade", None, "inst", None), P("blade", None, "inst", None))
    return jax.shard_map(
        on_device, mesh=mesh, in_specs=in_specs, out_specs=out_specs, check_vma=False
    )
```

```python
import math

import jax
import jax.numpy as jnp
from jax import lax
from jax.experimental import pallas as pl
from jax.experimental.pallas import tpu as pltpu
from jax.sharding import PartitionSpec as P

SNAPS = 24
NH = 11
NV = 5
OWN = 12
OMEGA = 0.15
SUB, LANE = 8, 128
ROWS = NV * OWN
FIELD = 2 * ROWS
FACE_ROWS = 5 * OWN // 2
MPITCH = OWN * 32 + 8
CHUNKS = 2
CHUNK = OWN // CHUNKS
OUT_CHUNKS = 3
OUT_CHUNK = OWN // OUT_CHUNKS


def derivative_weights():
    weights = [0.0]
    for n in range(1, 12):
        total = sum(k * math.sin(2 * math.pi * ((k * n) % SNAPS) / SNAPS) for k in range(1, NH + 1))
        weights.append(-(2.0 / SNAPS) * total)
    return weights


DERIV = derivative_weights()


def exchanged(block, late):
    count, cores = lax.axis_size("blade"), lax.axis_size("inst")
    route = []
    for i in range(count):
        for core in range(cores):
            partner = (i + 1 if (i + late) % 2 == 0 else i - 1) % count
            route.append((i * cores + core, partner * cores + core))
    return lax.ppermute(block, ("blade", "inst"), route)


def first_face():
    return lax.axis_index("blade") % 2


def lanes():
    return lax.broadcasted_iota(jnp.int32, (SUB, LANE), 1)


def sublanes():
    return lax.broadcasted_iota(jnp.int32, (SUB, LANE), 0)


def take(x, index):
    return jnp.take_along_axis(x, index, axis=1, mode="promise_in_bounds")


def quarters(row):
    first = jnp.broadcast_to(row[:, :LANE], (SUB, LANE))
    second = jnp.broadcast_to(row[:, LANE:], (SUB, LANE))
    sub = sublanes()
    both = jnp.where(sub < 4, first, second)
    return take(both, 32 * (sub & 3) + (lanes() & 31))


def wide(row):
    return jnp.concatenate([row[:, LANE * k : LANE * (k + 1)] for k in range(SUB)], axis=0)


def load_blocks(blocks, scratch, t):
    for k in range(SUB):
        tile = blocks[0, t, :, LANE * k : LANE * (k + 1)].astype(jnp.float32)
        scratch[pl.ds(pl.multiple_of(k * MPITCH + t * 32, 8), NV * NV), :] = tile


def fetch(pairs, sems):
    copies = [pltpu.make_async_copy(src, dst, sems.at[n]) for n, (src, dst) in enumerate(pairs)]
    for copy in copies:
        copy.start()
    return copies


def fetch_blocks(blocks, scratch, sems):
    return fetch(
        [(blocks.at[:, pl.ds(CHUNK * n, CHUNK)], scratch.at[:, pl.ds(CHUNK * n, CHUNK)]) for n in range(CHUNKS)],
        sems,
    )


def block_row(scratch, t, ij):
    return scratch[pl.ds(t * 32 + ij, SUB, stride=MPITCH), :]


def packed(parts, quarter):
    result = parts[-1]
    for g in reversed(range(len(parts) - 1)):
        result = jnp.where(quarter == g, parts[g], result)
    return result


def phase_weights(phase, rho):
    shape = (16, LANE)
    order = lax.broadcasted_iota(jnp.int32, shape, 0) + 1
    lag = lax.broadcasted_iota(jnp.int32, shape, 1)
    padded = jnp.concatenate([phase[...], jnp.zeros((1, LANE - NH), jnp.int32)], axis=1)
    spread = jnp.where(lag == order - 1, jnp.broadcast_to(padded, shape), 0).astype(jnp.float32)
    index = jnp.sum(spread, axis=1, keepdims=True)
    turns = (32 * order * (lag & 31)).astype(jnp.float32) - 3.0 * index
    turns = turns - 768.0 * jnp.floor(turns * (1.0 / 768.0) + 0.5)
    waves = jnp.where(order <= NH, jnp.cos(turns * (2.0 * math.pi / 768.0)), 0.0)
    parity = (1 - (lag[:1] & 1)).astype(jnp.float32)
    row = (2.0 / SNAPS) * (parity + jnp.sum(waves, axis=0, keepdims=True))
    for n in range(SNAPS):
        value = jnp.broadcast_to(row[:, n : n + 1], (SUB, LANE))
        rho[0, (-n) % SNAPS] = value
        rho[1, n] = value


def dual_kernel(
    phase, tangent, adjoint, precond, up_weight, lo_weight, up_cells, lo_cells,
    out, m_s, rho, index, scale, p_v, a_v, ph, uw, lw, uc, lc, t_sem, p_sem, w_sem,
):
    small = fetch(
        [(phase, ph), (up_weight, uw), (lo_weight, lw), (up_cells, uc), (lo_cells, lc)], w_sem
    )
    seeds = fetch([(adjoint, a_v), (tangent, out.at[pl.ds(0, ROWS)])], t_sem)
    chunks = fetch_blocks(precond, p_v, p_sem)
    for copy in small:
        copy.wait()
    phase_weights(ph, rho)
    index[0] = quarters(uc[...]) & (LANE - 1)
    index[1] = quarters(lc[...]) & (LANE - 1)
    up_scale = quarters(uw[...])
    lo_scale = quarters(lw[...])
    quarter = lanes() >> 5
    scale[0] = up_scale
    scale[1] = lo_scale
    scale[2] = jnp.where(quarter == 0, 1.0, up_scale)
    scale[3] = jnp.where(quarter == 1, 1.0, lo_scale)
    scale[4] = jnp.where(quarter == 0, lo_scale, 1.0)
    scale[5] = jnp.where(quarter == 1, up_scale, 1.0)

    def apply(t):
        seed = [a_v[i * OWN + t] for i in range(NV)]
        for j in range(NV):
            total = block_row(m_s, t, j) * seed[0]
            for i in range(1, NV):
                total = total + block_row(m_s, t, i * NV + j) * seed[i]
            out[ROWS + j * OWN + t] = total

    seeds[0].wait()
    for t in range(OWN):
        if t % CHUNK == 0:
            chunks[t // CHUNK].wait()
        load_blocks(p_v, m_s, t)
        if t > 0:
            apply(t - 1)
    apply(OWN - 1)
    seeds[1].wait()


def early():
    return lax.axis_index("blade") < 2


def local_work(gathered, jacobian, upwind, out, m_s, mix):
    own = lax.axis_index("inst")

    for fld, sign in ((0, 1.0), (1, -1.0)):

        def mix_body(i, carry):
            base = (fld * NV + i) * OWN
            mine = [gathered[own, base + s] for s in range(OWN)]
            theirs = [gathered[1 - own, base + s] for s in range(OWN)]
            ring = mine + theirs
            for r in range(OWN):
                total = None
                for k in range(1, OWN):
                    term = (sign * OMEGA * DERIV[k]) * (ring[(r - k) % SNAPS] - ring[(r + k) % SNAPS])
                    total = term if total is None else total + term
                mix[base + r] = total
            return carry

        lax.fori_loop(0, NV, mix_body, 0)

    lane = lanes()
    cell = sublanes() * LANE + lane
    flow = jnp.where(cell == 0, 0.0, wide(upwind[...]))

    def body(t, carry):
        tangent = [gathered[own, i * OWN + t] for i in range(NV)]
        dual = [gathered[own, (NV + i) * OWN + t] for i in range(NV)]
        sums = [None] * NV
        dsums = [None] * NV
        for i in range(NV):
            for j in range(NV):
                m = block_row(m_s, t, i * NV + j)
                term = m * tangent[j]
                sums[i] = term if j == 0 else sums[i] + term
                term = m * dual[i]
                dsums[j] = term if i == 0 else dsums[j] + term
        for i in range(NV):
            x = pltpu.roll(tangent[i], 1, 1)
            x = jnp.where(lane == 0, pltpu.roll(x, 1, 0), x)
            out[i * OWN + t] = sums[i] - flow * x + mix[i * OWN + t]
            x = pltpu.roll(flow * dual[i], LANE - 1, 1)
            x = jnp.where(lane == LANE - 1, pltpu.roll(x, SUB - 1, 0), x)
            out[(NV + i) * OWN + t] = dsums[i] - x + mix[(NV + i) * OWN + t]
        return carry

    def prepare(t, carry):
        load_blocks(jacobian, m_s, t)
        return carry

    lax.fori_loop(0, OWN, prepare, 0)
    lax.fori_loop(0, OWN, body, 0)


def received(face, which, index, scale):
    lane = lanes()
    group = lane >> 2
    hit = take(index[1 - which], group) == lane
    spots = [group + 32 * (g + which * (1 - 2 * (g % 2))) for g in range(4)]
    full, mid = scale[1 - which], scale[4 + which]

    def terms(t):
        half, low = divmod(t, OWN // 2)
        parts = [face[t] * full, face[OWN + t] * mid, face[2 * OWN + low]]
        return [
            jnp.where(hit, take(parts[q // 4], spots[q % 4 + (2 * half if q >= 8 else 0)]), 0.0)
            for q in range(2 * NV)
        ]

    return terms


def local_kernel(gathered, jacobian, upwind, given, ahead, index, scale, out, m_s, mix):
    @pl.when(jnp.logical_not(early()))
    def _():
        local_work(gathered, jacobian, upwind, out, m_s, mix)

    terms = received(ahead, 1 - first_face(), index, scale)
    for t in range(OWN):
        for q, term in enumerate(terms(t)):
            out[q * OWN + t] = out[q * OWN + t] - term


def rotate_kernel(
    gathered, jacobian, upwind, rho, index, scale, ahead, after, partial, f_s, m_s, mix
):
    own = lax.axis_index("inst")
    first = first_face()
    quarter = lanes() >> 5
    odd = (quarter & 1) == 1
    even_rows = jnp.where(odd, index[1], index[0])
    odd_rows = jnp.where(odd, index[0], index[1])

    for n in range(SNAPS):
        core, t = (own, n) if n < OWN else (1 - own, n - OWN)
        rows = [
            take(gathered[core, q * OWN + t], odd_rows if q % 2 else even_rows)
            for q in range(2 * NV)
        ]
        for side in range(2):
            order = [rows[q ^ side] for q in range(2 * NV)]
            f_s[side, 0, n] = packed(order[:4], quarter)
            f_s[side, 1, n] = packed(order[4:8], quarter)
            f_s[side, 2, n] = jnp.where(odd, order[9], order[8])

    for result, which in ((ahead, first), (after, 1 - first)):
        for j in range(3):
            sums = [None] * OWN
            for s in range(SNAPS):
                x = f_s[which, j, s]
                for r in range(OWN):
                    term = rho[which, (r - s) % SNAPS] * x
                    sums[r] = term if sums[r] is None else sums[r] + term
            if j == 0:
                for r in range(OWN):
                    result[r] = sums[r]
            elif j == 1:
                for r in range(OWN):
                    result[OWN + r] = sums[r] * scale[2 + which]
            else:
                for r in range(OWN // 2):
                    both = jnp.where(quarter < 2, sums[r], sums[r + OWN // 2])
                    result[2 * OWN + r] = both * scale[which]

    @pl.when(early())
    def _():
        local_work(gathered, jacobian, upwind, partial, m_s, mix)


def final_kernel(
    partial, after, m_s, index, scale, tangent_out, adjoint_out, t_v, a_v, o_sem
):
    terms = received(after, first_face(), index, scale)

    def apply(t):
        rows = [partial[q * OWN + t] - term for q, term in enumerate(terms(t))]
        for i in range(NV):
            total = block_row(m_s, t, i * NV) * rows[0]
            for j in range(1, NV):
                total = total + block_row(m_s, t, i * NV + j) * rows[j]
            t_v[i, t] = total
            a_v[i, t] = rows[NV + i]

    copies = []
    for n in range(OUT_CHUNKS):
        span = pl.ds(OUT_CHUNK * n, OUT_CHUNK)
        for t in range(OUT_CHUNK * n, OUT_CHUNK * (n + 1)):
            apply(t)
        for side, (src, dst) in enumerate(((t_v, tangent_out), (a_v, adjoint_out))):
            copy = pltpu.make_async_copy(src.at[:, span], dst.at[:, span], o_sem.at[2 * n + side])
            copy.start()
            copies.append(copy)
    for copy in copies:
        copy.wait()


def rows_of(count):
    return jax.ShapeDtypeStruct((count, SUB, LANE), jnp.float32)


BLOCK = (SUB * MPITCH, LANE)
BLOCKS = jax.ShapeDtypeStruct(BLOCK, jnp.float32)
HBM = pl.BlockSpec(memory_space=pltpu.HBM)
VMEM = pl.BlockSpec(memory_space=pltpu.VMEM)


def held(shape, dtype=jnp.float32):
    return pltpu.VMEM(shape, dtype)


def sems(count):
    return pltpu.SemaphoreType.DMA((count,))


def call(kernel, in_specs, out_shape, scratch, name, aliases={}, **kinds):
    return pl.pallas_call(
        kernel,
        in_specs=in_specs,
        out_shape=out_shape,
        scratch_shapes=scratch,
        input_output_aliases=aliases,
        compiler_params=pltpu.CompilerParams(vmem_limit_bytes=24 << 20),
        name=name,
        **kinds,
    )


def on_device(
    tangent_seed,
    adjoint_seed,
    jacobian,
    precond,
    upwind,
    up_weight,
    bottom_face_strength,
    up_cells,
    lo_cells,
    phase_index,
):
    face = up_cells.shape[0]
    tables = (phase_index.reshape(1, phase_index.shape[0]), up_weight, bottom_face_strength, up_cells.reshape(1, face), lo_cells.reshape(1, face))
    rows = (ROWS, SUB, LANE)
    both = (2, FIELD, SUB, LANE)
    fields, precond_rows, rho, index, scale = call(
        dual_kernel,
        [HBM] * 8,
        (
            rows_of(FIELD),
            BLOCKS,
            jax.ShapeDtypeStruct((2, SNAPS, SUB, LANE), jnp.float32),
            jax.ShapeDtypeStruct((2, SUB, LANE), jnp.int32),
            rows_of(6),
        ),
        [
            held(precond.shape, precond.dtype),
            held(rows),
            held(tables[0].shape, jnp.int32),
            held((1, face)),
            held((1, face)),
            held((1, face), jnp.int32),
            held((1, face), jnp.int32),
            sems(2),
            sems(CHUNKS),
            sems(5),
        ],
        "dual",
    )(
        *[
            pltpu.with_memory_space_constraint(x, pltpu.HBM)
            for x in (tables[0], tangent_seed.reshape(rows), adjoint_seed.reshape(rows), precond, *tables[1:])
        ],
    )
    gathered = lax.all_gather(fields, "inst", axis=0, tiled=True).reshape(both)
    local_scratch = [held(BLOCK), held((FIELD, SUB, LANE))]
    ahead, after, partial = call(
        rotate_kernel,
        [VMEM] * 6,
        (rows_of(FACE_ROWS), rows_of(FACE_ROWS), rows_of(FIELD)),
        [held((2, 3, SNAPS, SUB, LANE)), *local_scratch],
        "rotate",
    )(gathered, jacobian, upwind, rho, index, scale)
    ahead = exchanged(ahead, 0)
    after = exchanged(after, 1)
    partial = call(
        local_kernel, [VMEM] * 7, rows_of(FIELD), local_scratch, "local", {3: 0}
    )(gathered, jacobian, upwind, partial, ahead, index, scale)
    out = (NV, OWN, SUB, LANE)
    tangent_out, adjoint_out = call(
        final_kernel,
        [VMEM] * 5,
        (jax.ShapeDtypeStruct(out, jnp.float32), jax.ShapeDtypeStruct(out, jnp.float32)),
        [held(out), held(out), sems(2 * OUT_CHUNKS)],
        "final",
        out_specs=(HBM, HBM),
    )(partial, after, precond_rows, index, scale)
    return tangent_out.reshape(tangent_seed.shape), adjoint_out.reshape(adjoint_seed.shape)


def solution(mesh):
    in_specs = (
        P("blade", None, "inst", None),
        P("blade", None, "inst", None),
        P("blade", "inst", None, None),
        P("blade", "inst", None, None),
        P("blade", None),
        P("blade", None),
        P("blade", None),
        P(),
        P(),
        P(),
    )
    out_specs = (P("blade", None, "inst", None), P("blade", None, "inst", None))
    return jax.shard_map(
        on_device, mesh=mesh, in_specs=in_specs, out_specs=out_specs, check_vma=False
    )
```
